32 devices in a mesh: blk: 4 (over y, x), py: 4 (over z), pz: 2 (over core).
Axes of the slice: x: 2, y: 2, z: 4, core: 2. Of those that a mesh axis runs over, the one named last changes fastest.
Arguments:
- source: float32 [256, 1024, 128], P(('py', 'pz'), 'blk'), may hold values from -6 to 6
- conduct: float32 [3], replicated, may hold values from 0.3 to 3
- neighbours: int32 [4, 2], replicated, may hold values from -1 to 3, as said below
- orient: int32 [4], replicated, may hold values 0 or 1
Outputs:
- solution: float32 [256, 1024, 128], P(('py', 'pz'), 'blk')
- norms: float32 [3], replicated
The draws below stay inside these ranges and needn't reach their ends.
Inputs may be any that keep to these rules, and one draw needn't show every extreme that they name: `neighbours`: the blocks form one chain: row b holds the left and the right neighbour of block b, -1 marks the two ends, and a block is the left neighbour of its right neighbour.
All inputs are finite; a program needn't handle non-finite values.
Results may differ from the reference program's by a relative error of at most 0.00011.
Values sent between devices are 32-bit elements; how exact they have to be, the bound alone decides.
A program may use at most 128 MiB of HBM per device.

```python
import math
import jax
import jax.numpy as jnp
from jax import lax

NY = 256
NZ = 128
BX = 256
OV = 64
ITERS = 3
EXT = 384
BLOCKS = 4
CHAIN = 1024


def draw_neighbours(key, part):
    own_key = jax.random.fold_in(key, 7919)
    scores = jax.random.randint(own_key, (BLOCKS,), 0, 1073741824, dtype=jnp.int32)
    block_ids = jnp.arange(BLOCKS, dtype=jnp.int32)
    before = (scores[None, :] < scores[:, None]) | (scores[None, :] == scores[:, None]) & (block_ids[None, :] < block_ids[:, None])
    position = jnp.sum(before.astype(jnp.int32), axis=1).astype(jnp.int32)
    prev_match = position[None, :] == (position - 1)[:, None]
    next_match = position[None, :] == (position + 1)[:, None]
    previous_id = jnp.sum(jnp.where(prev_match, block_ids[None, :], 0), axis=1).astype(jnp.int32)
    following_id = jnp.sum(jnp.where(next_match, block_ids[None, :], 0), axis=1).astype(jnp.int32)
    previous = jnp.where(position > 0, previous_id, -1)
    following = jnp.where(position < BLOCKS - 1, following_id, -1)
    return jnp.stack([previous, following], axis=1).astype(jnp.int32)


def place_ends(values, rng, low, high):
    extent = values.shape
    place = [jax.random.randint(jax.random.fold_in(rng, axis), (), 0, extent[axis]) for axis in range(len(extent))]
    values = values.at[tuple(place)].set(low)
    longest = extent.index(max(extent))
    place[longest] = (place[longest] + 1) % extent[longest]
    return values.at[tuple(place)].set(high)


def shard_levels(key, dims, split, low, high):
    def one(dim, parts):
        heights = jax.random.uniform(jax.random.fold_in(jax.random.fold_in(key, 6), dim), (parts,), jnp.float32, low / len(split), high / len(split))
        return jnp.repeat(jnp.exp(heights), dims[dim] // parts).reshape((-1,) + (1,) * (len(dims) - dim - 1))

    gain = one(*split[0])
    for cut in split[1:]:
        gain = gain * one(*cut)
    return gain


def gaussian(key, dims, width, reach, cuts=(), kind=jnp.bfloat16):
    array = width * jax.random.normal(key, dims, jnp.float32)
    if cuts:
        array = array * shard_levels(key, dims, cuts, -0.22, 0.18)
    return jnp.clip(array, -reach, reach).astype(kind)


def setup_inputs(seed: int = 0) -> dict:
    splits = jax.random.split(jax.random.key(seed), 5)
    source = gaussian(splits[0], (NY, CHAIN, NZ), 1.0, 6.0, ((0, 8), (1, 4)), jnp.float32)
    conduct = jnp.clip(jnp.exp(jax.random.uniform(splits[1], (3,), jnp.float32, math.log(0.3), math.log(3.0))), 0.3, 3.0)
    neighbours = draw_neighbours(jax.random.fold_in(splits[4], 71), 0)
    orient = place_ends((jax.random.randint(splits[3], (BLOCKS,), 0, 2) < 1).astype(jnp.int32), jax.random.fold_in(splits[3], 1), 0, 1)
    return dict(source=source, conduct=conduct, neighbours=neighbours, orient=orient)


HIGHEST = lax.Precision.HIGHEST

def sine_basis(row_index, col_index, length):
    product = (row_index[:, None] + 1) * (col_index[None, :] + 1) % (2 * (length + 1))
    angles = jnp.pi * product.astype(jnp.float32) / (length + 1)
    return (jnp.sqrt(2.0 / (length + 1)) * jnp.sin(angles)).astype(jnp.float32)

def spectrum(index, length):
    angles = jnp.pi * (index.astype(jnp.float32) + 1.0) / (2.0 * (length + 1))
    return (4.0 * jnp.sin(angles) ** 2).astype(jnp.float32)

def apply_operator(extended, conduct):
    centre = extended[:, 1:-1, :]
    padded = jnp.pad(centre, ((1, 1), (0, 0), (1, 1)))
    along = 2.0 * centre - extended[:, :-2, :] - extended[:, 2:, :]
    across = 2.0 * centre - padded[:-2, :, 1:-1] - padded[2:, :, 1:-1]
    depth = 2.0 * centre - padded[1:-1, :, :-2] - padded[1:-1, :, 2:]
    return conduct[0] * along + conduct[1] * across + conduct[2] * depth

def block_solve(residual, plane_basis, row_basis, depth_basis, spectra):
    modes = jnp.einsum('yxz,xk->ykz', residual, plane_basis, precision=HIGHEST)
    modes = jnp.einsum('yxz,yk->kxz', modes, row_basis, precision=HIGHEST)
    modes = jnp.einsum('yxz,zk->yxk', modes, depth_basis, precision=HIGHEST)
    modes = modes / spectra
    modes = jnp.einsum('yxz,zk->yxk', modes, depth_basis, precision=HIGHEST)
    modes = jnp.einsum('kxz,yk->yxz', modes, row_basis, precision=HIGHEST)
    return jnp.einsum('ykz,xk->yxz', modes, plane_basis, precision=HIGHEST)

def reference(source, conduct, neighbours, orient):
    blocks = neighbours.shape[0]
    plane_ids = jnp.arange(EXT, dtype=jnp.int32)
    row_ids = jnp.arange(NY, dtype=jnp.int32)
    depth_ids = jnp.arange(NZ, dtype=jnp.int32)
    plane_basis = sine_basis(plane_ids, plane_ids, EXT)
    row_basis = sine_basis(row_ids, row_ids, NY)
    depth_basis = sine_basis(depth_ids, depth_ids, NZ)
    spectra = conduct[0] * spectrum(plane_ids, EXT)[None, :, None] + conduct[1] * spectrum(row_ids, NY)[:, None, None] + conduct[2] * spectrum(depth_ids, NZ)[None, None, :]
    sources = []
    for block in range(blocks):
        piece = source[:, block * BX:(block + 1) * BX, :]
        sources.append(jnp.where(orient[block] == 1, piece[:, ::-1, :], piece))
    source_stack = jnp.stack(sources)
    iterates = [jnp.zeros((NY, BX, NZ), jnp.float32) for block in range(blocks)]
    plane_pos = jnp.arange(EXT, dtype=jnp.int32)
    cell_count = float(blocks * BX * NY * NZ)
    norm_list = []
    for iteration in range(ITERS):
        iterate_stack = jnp.stack(iterates)
        updated = []
        squares = jnp.zeros((), jnp.float32)
        for block in range(blocks):
            left_id = neighbours[block, 0]
            right_id = neighbours[block, 1]
            has_left = (left_id >= 0).astype(jnp.float32)
            has_right = (right_id >= 0).astype(jnp.float32)
            left_safe = jnp.maximum(left_id, 0)
            right_safe = jnp.maximum(right_id, 0)
            extended = jnp.concatenate([iterate_stack[left_safe][:, BX - OV - 1:, :] * has_left, iterates[block], iterate_stack[right_safe][:, :OV + 1, :] * has_right], axis=1)
            source_ext = jnp.concatenate([source_stack[left_safe][:, BX - OV:, :] * has_left, sources[block], source_stack[right_safe][:, :OV, :] * has_right], axis=1)
            plane_mask = jnp.where(plane_pos < OV, has_left, jnp.where(plane_pos >= OV + BX, has_right, 1.0))
            residual = (source_ext - apply_operator(extended, conduct)) * plane_mask[None, :, None]
            squares = squares + jnp.sum(residual[:, OV:OV + BX, :] ** 2)
            correction = block_solve(residual, plane_basis, row_basis, depth_basis, spectra)
            updated.append(iterates[block] + correction[:, OV:OV + BX, :])
        norm_list.append(jnp.sqrt(squares / cell_count))
        iterates = updated
    placed = [jnp.where(orient[block] == 1, iterates[block][:, ::-1, :], iterates[block]) for block in range(blocks)]
    return (jnp.concatenate(placed, axis=1), jnp.stack(norm_list).astype(jnp.float32))
```

```python
import jax
import jax.numpy as jnp
import numpy as np
from jax import lax
from jax.sharding import PartitionSpec as P

OV = 64
ITERS = 3

HIGHEST = lax.Precision.HIGHEST
HIGH = lax.Precision.HIGH


def sine_basis(row_index, col_index, length):
    product = (row_index[:, None] + 1) * (col_index[None, :] + 1) % (2 * (length + 1))
    values = np.sqrt(2.0 / (length + 1)) * np.sin(np.pi * product / (length + 1))
    return values.astype(np.float32)


def spectrum(length):
    angles = np.pi * (np.arange(length) + 1.0) / (2.0 * (length + 1))
    return (4.0 * np.sin(angles) ** 2).astype(np.float32)


def plane_tables(planes):
    ids = np.arange(planes)
    small = np.arange(OV - 1)
    own = sine_basis(ids, ids, planes)
    margin = sine_basis(small, small, OV - 1)
    count = planes + 2 * (OV - 1) + 2
    at_tail = planes
    at_head = planes + OV - 1
    forward = np.zeros((planes, count), np.float32)
    forward[:, :planes] = own
    forward[planes - OV : planes - 1, at_tail:at_head] = margin
    forward[1:OV, at_head : at_head + OV - 1] = margin
    forward[planes - 1, count - 2] = 1.0
    forward[0, count - 1] = 1.0
    mu = np.ones((count,), np.float32)
    mu[:planes] = spectrum(planes)
    mu[at_tail:at_head] = spectrum(OV - 1)
    mu[at_head : at_head + OV - 1] = spectrum(OV - 1)
    box_pick = np.zeros((count, 4), np.float32)
    box_pick[:planes, 0] = own[0]
    box_pick[:planes, 1] = own[-1]
    margin_pick = np.zeros((count, 4), np.float32)
    margin_pick[at_tail:at_head, 2] = margin[-1]
    margin_pick[at_head : at_head + OV - 1, 3] = margin[0]
    return own, forward, mu, box_pick, margin_pick


def shift_blocks(values, ids):
    blocks = ids.shape[0]
    match = (ids[:, None] == jnp.arange(blocks, dtype=jnp.int32)[None, :]).astype(jnp.float32)
    rows = []
    for b in range(blocks):
        total = match[b, 0] * values[0]
        for other in range(1, blocks):
            total = total + match[b, other] * values[other]
        rows.append(total)
    return jnp.stack(rows)


def shards(source, conduct, neighbours, orient):
    blocks = neighbours.shape[0]
    rows, planes, depth = source.shape
    group = lax.axis_size("py") * lax.axis_size("pz")
    all_rows = rows * group
    own_depth = depth // group
    own_block = lax.axis_index("blk")
    member = lax.axis_index("py") * lax.axis_size("pz") + lax.axis_index("pz")
    chosen = jnp.arange(blocks, dtype=jnp.int32) == own_block
    flipped = jnp.sum(jnp.where(chosen, orient, 0)) == 1
    c0, c1, c2 = conduct[0], conduct[1], conduct[2]

    own, forward, mu_plane, box_pick, margin_pick = plane_tables(planes)
    count = forward.shape[1]
    row_ids = np.arange(all_rows)
    local_ids = np.arange(rows)
    depth_ids = np.arange(depth)
    row_basis = jnp.asarray(sine_basis(row_ids, row_ids, all_rows))
    local_basis = jnp.asarray(sine_basis(local_ids, local_ids, rows))
    depth_basis = jnp.asarray(sine_basis(depth_ids, depth_ids, depth))
    beside = np.stack([rows * np.arange(group) - 1, rows * (np.arange(group) + 1)], axis=1)
    beside_basis = sine_basis(beside.reshape(-1), row_ids, all_rows)
    beside_basis = beside_basis.reshape(group, 2, all_rows)
    beside_basis[0, 0] = 0.0
    beside_basis[-1, 1] = 0.0
    beside_basis = jnp.asarray(beside_basis)
    mu_row = jnp.asarray(spectrum(all_rows))
    mu_local = jnp.asarray(spectrum(rows))
    mu_depth = jnp.asarray(spectrum(depth))
    mu_plane = jnp.asarray(mu_plane)
    own_table = jnp.asarray(own)
    first_col, last_col = own_table[0], own_table[-1]
    forward = jnp.asarray(forward)
    forward = jnp.where(flipped, forward[::-1], forward)
    backward = jnp.where(flipped, own_table[::-1], own_table)
    pick = jnp.asarray(box_pick) + c0 * jnp.asarray(margin_pick)

    cells = jnp.einsum("ypz,zk->ypk", source, depth_basis, precision=HIGH)
    cells = jnp.einsum("ypk,pi->yik", cells, forward, precision=HIGH)
    modes = jnp.einsum("yik,ym->mik", cells, local_basis, precision=HIGH)
    slab_spectra = (
        c0 * mu_plane[None, :, None]
        + c1 * mu_local[:, None, None]
        + c2 * mu_depth[None, None, :]
    )
    slab = modes / slab_spectra
    edges = jnp.einsum("mik,em->eki", slab, local_basis[jnp.array([0, rows - 1])], precision=HIGH)
    ends = jnp.einsum("mik,iq->mqk", slab, pick, precision=HIGH)
    ends = jnp.einsum("mqk,ym->kqy", ends, local_basis, precision=HIGH)
    plain = jnp.zeros((2, rows, depth), jnp.float32)
    plain = jnp.concatenate([plain, jnp.stack([cells[:, count - 2], cells[:, count - 1]])], axis=0)
    ends = ends + jnp.transpose(plain, (2, 0, 1))

    packed = jnp.concatenate([edges[0], edges[1], ends.reshape(depth, 4 * rows)], axis=1)
    packed = lax.all_to_all(packed, ("py", "pz"), split_axis=0, concat_axis=0, tiled=True)
    packed = packed.reshape(group, own_depth, 2 * count + 4 * rows)
    edge_first = packed[:, :, :count]
    edge_last = packed[:, :, count : 2 * count]
    ends = packed[:, :, 2 * count :].reshape(group, own_depth, 4, rows)

    empty = jnp.zeros_like(edge_first[:1])
    below = jnp.concatenate([empty, edge_last[:-1]], axis=0)
    above = jnp.concatenate([edge_first[1:], empty], axis=0)
    first_rows = row_basis[rows * np.arange(group)]
    last_rows = row_basis[rows * np.arange(group) + rows - 1]
    seam_basis = jnp.concatenate([first_rows, last_rows], axis=0)
    seams = jnp.concatenate([below, above], axis=0)
    joined = c1 * jnp.einsum("rki,rj->kji", seams, seam_basis, precision=HIGH)
    held_depth = lax.dynamic_slice_in_dim(mu_depth, member * own_depth, own_depth)
    cross = c1 * mu_row[None, :] + c2 * held_depth[:, None]
    spectra = c0 * mu_plane[None, None, :] + cross[:, :, None]
    moments = jnp.einsum("kji,iq->qkj", joined / spectra, pick, precision=HIGH)
    moments = moments + jnp.einsum(
        "dkqy,dyj->qkj", ends, row_basis.reshape(group, rows, all_rows), precision=HIGHEST
    )
    every = lax.all_gather(moments, "blk", axis=0)

    half = 0.5 * jnp.sqrt(cross / c0)
    root = jnp.sqrt(1.0 + half * half)
    theta = 2.0 * jnp.log1p(half + half * half / (1.0 + root))
    sinh = 2.0 * half * root

    def tanh_of(n):
        decay = jnp.exp(-2.0 * n * theta)
        return -jnp.expm1(-2.0 * n * theta) / (1.0 + decay)

    outer = 1.0 / tanh_of(float(OV))
    mid = tanh_of(0.5 * (planes + 1))
    even_inv = 1.0 / (sinh * (outer + mid))
    odd_inv = 1.0 / (sinh * (outer + 1.0 / mid))
    reach = jnp.exp(-(planes + 1.0) * theta)
    span = -jnp.expm1(-2.0 * (planes + 1.0) * theta)
    beta = sinh * 2.0 * reach / span
    alpha = jnp.exp(-theta) * -jnp.expm1(-2.0 * planes * theta) / span

    left_ids, right_ids = neighbours[:, 0], neighbours[:, 1]
    own_low, own_high = every[:, 0], every[:, 1]
    beyond_low = shift_blocks(every[:, 2], left_ids) / c0
    beyond_high = shift_blocks(every[:, 3], right_ids) / c0
    push_low = jnp.zeros_like(own_low)
    push_high = jnp.zeros_like(own_low)
    squares = [jnp.sum(source * source)]
    for iteration in range(ITERS):
        drive_low = beyond_low + own_low
        drive_high = beyond_high + own_high
        even = (drive_low + drive_high) * even_inv
        odd = (drive_low - drive_high) * odd_inv
        low = 0.5 * (even + odd)
        high = 0.5 * (even - odd)
        push_low = push_low + low
        push_high = push_high + high
        if iteration == ITERS - 1:
            break
        inner_low = own_low + alpha * low + beta * high
        inner_high = own_high + beta * low + alpha * high
        jump_low = shift_blocks(inner_high, left_ids) - low
        jump_high = shift_blocks(inner_low, right_ids) - high
        held = jnp.where(chosen[:, None, None], jump_low**2 + jump_high**2, 0.0)
        squares.append(c0 * c0 * jnp.sum(held))
        push_low = push_low + jump_low
        push_high = push_high + jump_high
        own_low = alpha * jump_low + beta * jump_high
        own_high = beta * jump_low + alpha * jump_high
        beyond_low = shift_blocks(jump_high, left_ids)
        beyond_high = shift_blocks(jump_low, right_ids)
    pushes = c0 * jnp.stack([push_low, push_high], axis=1)
    pushes = jnp.sum(jnp.where(chosen[:, None, None, None], pushes, 0.0), axis=0)

    total = (
        joined[:, :, :planes]
        + pushes[0][:, :, None] * first_col
        + pushes[1][:, :, None] * last_col
    )
    total = total / spectra[:, :, :planes]
    beside_values = jnp.einsum("kji,dsj->dksi", total, beside_basis, precision=HIGH)
    beside_values = beside_values + jnp.stack([below, above], axis=2)[:, :, :, :planes]
    pushes = jnp.einsum(
        "skj,dyj->dksy", pushes, row_basis.reshape(group, rows, all_rows), precision=HIGHEST
    )
    packed = jnp.concatenate(
        [
            beside_values.reshape(group, own_depth, 2 * planes),
            pushes.reshape(group, own_depth, 2 * rows),
        ],
        axis=2,
    ).reshape(depth, 2 * planes + 2 * rows)
    packed = lax.all_to_all(packed, ("py", "pz"), split_axis=0, concat_axis=0, tiled=True)
    packed = jnp.transpose(packed)
    below = packed[:planes]
    above = packed[planes : 2 * planes]
    pushes = jnp.einsum(
        "syk,ym->smk",
        packed[2 * planes :].reshape(2, rows, depth),
        local_basis,
        precision=HIGHEST,
    )

    modes = (
        modes[:, :planes]
        + c1 * local_basis[0][:, None, None] * below
        + c1 * local_basis[-1][:, None, None] * above
        + first_col[None, :, None] * pushes[0][:, None, :]
        + last_col[None, :, None] * pushes[1][:, None, :]
    ) / slab_spectra[:, :planes]
    cells = jnp.einsum("mik,ym->yik", modes, local_basis, precision=HIGH)
    cells = jnp.einsum("yik,pi->ypk", cells, backward, precision=HIGH)
    solution = jnp.einsum("ypk,zk->ypz", cells, depth_basis, precision=HIGH)

    cell_count = float(blocks * planes * all_rows * depth)
    sums = lax.psum(jnp.stack(squares), ("blk", "py", "pz"))
    return (solution, jnp.sqrt(sums / cell_count))


def solution(mesh):
    placed = (P(("py", "pz"), "blk", None), P(), P(), P())
    return jax.shard_map(
        shards,
        mesh=mesh,
        in_specs=placed,
        out_specs=(P(("py", "pz"), "blk", None), P()),
        check_vma=False,
    )
```

```python
import functools
import jax
import jax.numpy as jnp
import numpy as np
from jax import lax
from jax.experimental import pallas as pl
from jax.experimental.pallas import tpu as pltpu
from jax.sharding import PartitionSpec as P

OV = 64
ITERS = 3

HIGHEST = lax.Precision.HIGHEST
HIGH = lax.Precision.HIGH


def sine_basis(row_index, col_index, length):
    product = (row_index[:, None] + 1) * (col_index[None, :] + 1) % (2 * (length + 1))
    values = np.sqrt(2.0 / (length + 1)) * np.sin(np.pi * product / (length + 1))
    return values.astype(np.float32)


def spectrum(length):
    angles = np.pi * (np.arange(length) + 1.0) / (2.0 * (length + 1))
    return (4.0 * np.sin(angles) ** 2).astype(np.float32)


def plane_tables(planes):
    ids = np.arange(planes)
    small = np.arange(OV - 1)
    own = sine_basis(ids, ids, planes)
    margin = sine_basis(small, small, OV - 1)
    count = planes + 2 * (OV - 1) + 2
    at_tail = planes
    at_head = planes + OV - 1
    forward = np.zeros((planes, count), np.float32)
    forward[:, :planes] = own
    forward[planes - OV : planes - 1, at_tail:at_head] = margin
    forward[1:OV, at_head : at_head + OV - 1] = margin
    forward[planes - 1, count - 2] = 1.0
    forward[0, count - 1] = 1.0
    mu = np.ones((count,), np.float32)
    mu[:planes] = spectrum(planes)
    mu[at_tail:at_head] = spectrum(OV - 1)
    mu[at_head : at_head + OV - 1] = spectrum(OV - 1)
    box_pick = np.zeros((count, 4), np.float32)
    box_pick[:planes, 0] = own[0]
    box_pick[:planes, 1] = own[-1]
    margin_pick = np.zeros((count, 4), np.float32)
    margin_pick[at_tail:at_head, 2] = margin[-1]
    margin_pick[at_head : at_head + OV - 1, 3] = margin[0]
    return own, forward, mu, box_pick, margin_pick


def chain_kernel(planes, ids_ref, own_ref, c0_ref, theta_ref, sinh_ref, every_ref, push_ref, square_ref):
    blocks = every_ref.shape[0]
    c0 = c0_ref[0]
    theta = theta_ref[...]
    sinh = sinh_ref[...]
    far = jnp.exp(-2.0 * OV * theta)
    outer = (1.0 + far) / (1.0 - far)
    reach = jnp.exp(-(planes + 1.0) * theta)
    mid = (1.0 - reach) / (1.0 + reach)
    even_inv = 1.0 / (sinh * (outer + mid))
    odd_inv = 1.0 / (sinh * (outer + 1.0 / mid))
    span = 1.0 - reach * reach
    beta = 2.0 * sinh * reach / span
    alpha = jnp.exp(-theta) * (1.0 - jnp.exp(-2.0 * planes * theta)) / span
    masks = [
        [[(ids_ref[b, side] == o).astype(jnp.float32) for o in range(blocks)] for b in range(blocks)]
        for side in range(2)
    ]
    mine = [(own_ref[0] == b).astype(jnp.float32) for b in range(blocks)]

    def beside(values, side):
        shifted = []
        for b in range(blocks):
            total = masks[side][b][0] * values[0]
            for o in range(1, blocks):
                total = total + masks[side][b][o] * values[o]
            shifted.append(total)
        return shifted

    each = range(blocks)
    own_low = [every_ref[b, 0] for b in each]
    own_high = [every_ref[b, 1] for b in each]
    beyond_low = [v / c0 for v in beside([every_ref[b, 2] for b in each], 0)]
    beyond_high = [v / c0 for v in beside([every_ref[b, 3] for b in each], 1)]
    push_low = jnp.zeros_like(theta)
    push_high = jnp.zeros_like(theta)
    for iteration in range(ITERS):
        lows, highs, inner_lows, inner_highs = [], [], [], []
        for b in each:
            drive_low = beyond_low[b] + own_low[b]
            drive_high = beyond_high[b] + own_high[b]
            even = (drive_low + drive_high) * even_inv
            odd = (drive_low - drive_high) * odd_inv
            low = 0.5 * (even + odd)
            high = 0.5 * (even - odd)
            push_low = push_low + mine[b] * low
            push_high = push_high + mine[b] * high
            lows.append(low)
            highs.append(high)
            inner_lows.append(own_low[b] + alpha * low + beta * high)
            inner_highs.append(own_high[b] + beta * low + alpha * high)
        if iteration == ITERS - 1:
            break
        jump_low = [v - low for v, low in zip(beside(inner_highs, 0), lows)]
        jump_high = [v - high for v, high in zip(beside(inner_lows, 1), highs)]
        square = jnp.zeros_like(theta)
        for b in each:
            square = square + jump_low[b] * jump_low[b] + jump_high[b] * jump_high[b]
            push_low = push_low + mine[b] * jump_low[b]
            push_high = push_high + mine[b] * jump_high[b]
        square_ref[iteration] = square
        own_low = [alpha * jump_low[b] + beta * jump_high[b] for b in each]
        own_high = [beta * jump_low[b] + alpha * jump_high[b] for b in each]
        beyond_low = beside(jump_high, 0)
        beyond_high = beside(jump_low, 1)
    push_ref[0] = c0 * push_low
    push_ref[1] = c0 * push_high


def shards(source, conduct, neighbours, orient):
    blocks = neighbours.shape[0]
    rows, planes, depth = source.shape
    group = lax.axis_size("py") * lax.axis_size("pz")
    all_rows = rows * group
    own_depth = depth // group
    own_block = lax.axis_index("blk")
    member = lax.axis_index("py") * lax.axis_size("pz") + lax.axis_index("pz")
    chosen = jnp.arange(blocks, dtype=jnp.int32) == own_block
    flipped = jnp.sum(jnp.where(chosen, orient, 0)) == 1
    c0, c1, c2 = conduct[0], conduct[1], conduct[2]

    own, forward, mu_plane, box_pick, margin_pick = plane_tables(planes)
    count = forward.shape[1]
    row_ids = np.arange(all_rows)
    local_ids = np.arange(rows)
    depth_ids = np.arange(depth)
    row_basis = jnp.asarray(sine_basis(row_ids, row_ids, all_rows))
    local_basis = jnp.asarray(sine_basis(local_ids, local_ids, rows))
    depth_basis = jnp.asarray(sine_basis(depth_ids, depth_ids, depth))
    beside = np.stack([rows * np.arange(group) - 1, rows * (np.arange(group) + 1)], axis=1)
    beside_basis = sine_basis(beside.reshape(-1), row_ids, all_rows)
    beside_basis = beside_basis.reshape(group, 2, all_rows)
    beside_basis[0, 0] = 0.0
    beside_basis[-1, 1] = 0.0
    beside_basis = jnp.asarray(beside_basis)
    mu_row = jnp.asarray(spectrum(all_rows))
    mu_local = jnp.asarray(spectrum(rows))
    mu_depth = jnp.asarray(spectrum(depth))
    mu_plane = jnp.asarray(mu_plane)
    own_table = jnp.asarray(own)
    first_col, last_col = own_table[0], own_table[-1]
    forward = jnp.asarray(forward)
    forward = jnp.where(flipped, forward[::-1], forward)
    backward = jnp.where(flipped, own_table[::-1], own_table)
    pick = jnp.asarray(box_pick) + c0 * jnp.asarray(margin_pick)

    cells = jnp.einsum("ypz,zk->ypk", source, depth_basis, precision=HIGH)
    cells = jnp.einsum("ypk,ym->mpk", cells, local_basis, precision=HIGH)
    modes = jnp.einsum("mpk,pi->mik", cells, forward, precision=HIGH)
    slab_spectra = (
        c0 * mu_plane[None, :, None]
        + c1 * mu_local[:, None, None]
        + c2 * mu_depth[None, None, :]
    )
    slab = modes / slab_spectra
    edge_first = jnp.sum(slab * local_basis[0][:, None, None], axis=0)
    edge_last = jnp.sum(slab * local_basis[-1][:, None, None], axis=0)
    ends = jnp.einsum("mik,iq->mqk", slab, pick, precision=HIGHEST)
    plain = jnp.zeros((rows, 2, depth), jnp.float32)
    ends = ends + jnp.concatenate([plain, modes[:, count - 2 :]], axis=1)
    ends = jnp.einsum("mqk,ym->kqy", ends, local_basis, precision=HIGHEST)
    own_squares = jnp.sum(source * source)

    packed = jnp.concatenate(
        [
            jnp.transpose(edge_first),
            jnp.transpose(edge_last)[:, : count - 1],
            jnp.full((depth, 1), own_squares),
            ends.reshape(depth, 4 * rows),
        ],
        axis=1,
    )
    packed = lax.all_to_all(packed, ("py", "pz"), split_axis=0, concat_axis=0, tiled=True)
    packed = packed.reshape(group, own_depth, 2 * count + 4 * rows)
    edge_first = packed[:, :, :count]
    edge_last = packed[:, :, count : 2 * count]
    first_square = jnp.sum(packed[:, 0, 2 * count - 1])
    ends = packed[:, :, 2 * count :].reshape(group, own_depth, 4, rows)

    empty = jnp.zeros_like(edge_first[:1])
    below = jnp.concatenate([empty, edge_last[:-1]], axis=0)
    above = jnp.concatenate([edge_first[1:], empty], axis=0)
    first_rows = row_basis[rows * np.arange(group)]
    last_rows = row_basis[rows * np.arange(group) + rows - 1]
    seam_basis = jnp.concatenate([first_rows, last_rows], axis=0)
    seams = jnp.concatenate([below, above], axis=0)
    joined = c1 * jnp.einsum("rki,rj->kji", seams, seam_basis, precision=HIGHEST)
    held_depth = lax.dynamic_slice_in_dim(mu_depth, member * own_depth, own_depth)
    cross = c1 * mu_row[None, :] + c2 * held_depth[:, None]
    spectra = c0 * mu_plane[None, None, :] + cross[:, :, None]
    moments = jnp.einsum("kji,iq->qkj", joined / spectra, pick, precision=HIGHEST)
    moments = moments + jnp.einsum(
        "dkqy,dyj->qkj", ends, row_basis.reshape(group, rows, all_rows), precision=HIGHEST
    )
    shared = jnp.full((1,) + moments.shape[1:], first_square)
    every = lax.all_gather(jnp.concatenate([moments, shared], axis=0), "blk", axis=0)

    half = 0.5 * jnp.sqrt(cross / c0)
    root = jnp.sqrt(1.0 + half * half)
    theta = 2.0 * jnp.log1p(half + half * half / (1.0 + root))
    sinh = 2.0 * half * root
    in_smem = pl.BlockSpec(memory_space=pltpu.SMEM)
    in_vmem = pl.BlockSpec(memory_space=pltpu.VMEM)
    pushes, squares = pl.pallas_call(
        functools.partial(chain_kernel, planes),
        out_shape=(
            jax.ShapeDtypeStruct((2,) + theta.shape, jnp.float32),
            jax.ShapeDtypeStruct((ITERS - 1,) + theta.shape, jnp.float32),
        ),
        in_specs=[in_smem, in_smem, in_smem, in_vmem, in_vmem, in_vmem],
        out_specs=(in_vmem, in_vmem),
        name="chain",
    )(neighbours, own_block.reshape(1), c0.reshape(1), theta, sinh, every)
    squares = c0 * c0 * jnp.sum(squares, axis=(1, 2))

    total = (
        joined[:, :, :planes]
        + pushes[0][:, :, None] * first_col
        + pushes[1][:, :, None] * last_col
    )
    total = total / spectra[:, :, :planes]
    beside_values = jnp.einsum("kji,dsj->dksi", total, beside_basis, precision=HIGHEST)
    beside_values = beside_values + jnp.stack([below, above], axis=2)[:, :, :, :planes]
    pushes = jnp.einsum(
        "skj,dyj->dksy", pushes, row_basis.reshape(group, rows, all_rows), precision=HIGHEST
    )
    packed = jnp.concatenate(
        [
            beside_values.reshape(group, own_depth, 2 * planes),
            pushes.reshape(group, own_depth, 2 * rows),
            jnp.broadcast_to(squares, (group, own_depth, ITERS - 1)),
        ],
        axis=2,
    ).reshape(depth, 2 * planes + 2 * rows + ITERS - 1)
    packed = lax.all_to_all(packed, ("py", "pz"), split_axis=0, concat_axis=0, tiled=True)
    squares = packed[::own_depth, 2 * planes + 2 * rows :]
    packed = jnp.transpose(packed)
    below = packed[:planes]
    above = packed[planes : 2 * planes]
    pushes = jnp.einsum(
        "syk,ym->smk",
        packed[2 * planes : 2 * planes + 2 * rows].reshape(2, rows, depth),
        local_basis,
        precision=HIGHEST,
    )

    modes = (
        modes[:, :planes]
        + c1 * local_basis[0][:, None, None] * below
        + c1 * local_basis[-1][:, None, None] * above
        + first_col[None, :, None] * pushes[0][:, None, :]
        + last_col[None, :, None] * pushes[1][:, None, :]
    ) / slab_spectra[:, :planes]
    cells = jnp.einsum("mik,ym->yik", modes, local_basis, precision=HIGH)
    cells = jnp.einsum("yik,pi->ypk", cells, backward, precision=HIGH)
    solution = jnp.einsum("ypk,zk->ypz", cells, depth_basis, precision=HIGH)

    cell_count = float(blocks * planes * all_rows * depth)
    sums = jnp.concatenate([jnp.sum(every[:, 4, 0, 0])[None], jnp.sum(squares, axis=0)])
    return (solution, jnp.sqrt(sums / cell_count))


def solution(mesh):
    placed = (P(("py", "pz"), "blk", None), P(), P(), P())
    return jax.shard_map(
        shards,
        mesh=mesh,
        in_specs=placed,
        out_specs=(P(("py", "pz"), "blk", None), P()),
        check_vma=False,
    )
```

```python
import functools
import jax
import jax.numpy as jnp
import numpy as np
from jax import lax
from jax.experimental import pallas as pl
from jax.experimental.pallas import tpu as pltpu
from jax.sharding import PartitionSpec as P

OV = 64
ITERS = 3

HIGHEST = lax.Precision.HIGHEST
HIGH = lax.Precision.HIGH


def sine_basis(row_index, col_index, length):
    product = (row_index[:, None] + 1) * (col_index[None, :] + 1) % (2 * (length + 1))
    values = np.sqrt(2.0 / (length + 1)) * np.sin(np.pi * product / (length + 1))
    return values.astype(np.float32)


def spectrum(length):
    angles = np.pi * (np.arange(length) + 1.0) / (2.0 * (length + 1))
    return (4.0 * np.sin(angles) ** 2).astype(np.float32)


def plane_tables(planes):
    ids = np.arange(planes)
    small = np.arange(OV - 1)
    own = sine_basis(ids, ids, planes)
    margin = sine_basis(small, small, OV - 1)
    count = planes + 2 * (OV - 1) + 2
    at_tail = planes
    at_head = planes + OV - 1
    forward = np.zeros((planes, count), np.float32)
    forward[:, :planes] = own
    forward[planes - OV : planes - 1, at_tail:at_head] = margin
    forward[1:OV, at_head : at_head + OV - 1] = margin
    forward[planes - 1, count - 2] = 1.0
    forward[0, count - 1] = 1.0
    mu = np.ones((count,), np.float32)
    mu[:planes] = spectrum(planes)
    mu[at_tail:at_head] = spectrum(OV - 1)
    mu[at_head : at_head + OV - 1] = spectrum(OV - 1)
    box_pick = np.zeros((count, 4), np.float32)
    box_pick[:planes, 0] = own[0]
    box_pick[:planes, 1] = own[-1]
    margin_pick = np.zeros((count, 4), np.float32)
    margin_pick[at_tail:at_head, 2] = margin[-1]
    margin_pick[at_head : at_head + OV - 1, 3] = margin[0]
    return own, forward, mu, box_pick, margin_pick


def chain_kernel(planes, ids_ref, own_ref, c0_ref, theta_ref, sinh_ref, every_ref, push_ref, square_ref):
    blocks = every_ref.shape[0]
    c0 = c0_ref[0]
    theta = theta_ref[...]
    sinh = sinh_ref[...]
    far = jnp.exp(-2.0 * OV * theta)
    outer = (1.0 + far) / (1.0 - far)
    reach = jnp.exp(-(planes + 1.0) * theta)
    mid = (1.0 - reach) / (1.0 + reach)
    even_inv = 1.0 / (sinh * (outer + mid))
    odd_inv = 1.0 / (sinh * (outer + 1.0 / mid))
    span = 1.0 - reach * reach
    beta = 2.0 * sinh * reach / span
    alpha = jnp.exp(-theta) * (1.0 - jnp.exp(-2.0 * planes * theta)) / span
    masks = [
        [[(ids_ref[b, side] == o).astype(jnp.float32) for o in range(blocks)] for b in range(blocks)]
        for side in range(2)
    ]
    mine = [(own_ref[0] == b).astype(jnp.float32) for b in range(blocks)]

    def beside(values, side):
        shifted = []
        for b in range(blocks):
            total = masks[side][b][0] * values[0]
            for o in range(1, blocks):
                total = total + masks[side][b][o] * values[o]
            shifted.append(total)
        return shifted

    each = range(blocks)
    own_low = [every_ref[b, 0] for b in each]
    own_high = [every_ref[b, 1] for b in each]
    beyond_low = [v / c0 for v in beside([every_ref[b, 2] for b in each], 0)]
    beyond_high = [v / c0 for v in beside([every_ref[b, 3] for b in each], 1)]
    push_low = jnp.zeros_like(theta)
    push_high = jnp.zeros_like(theta)
    for iteration in range(ITERS):
        lows, highs, inner_lows, inner_highs = [], [], [], []
        for b in each:
            drive_low = beyond_low[b] + own_low[b]
            drive_high = beyond_high[b] + own_high[b]
            even = (drive_low + drive_high) * even_inv
            odd = (drive_low - drive_high) * odd_inv
            low = 0.5 * (even + odd)
            high = 0.5 * (even - odd)
            push_low = push_low + mine[b] * low
            push_high = push_high + mine[b] * high
            lows.append(low)
            highs.append(high)
            inner_lows.append(own_low[b] + alpha * low + beta * high)
            inner_highs.append(own_high[b] + beta * low + alpha * high)
        if iteration == ITERS - 1:
            break
        jump_low = [v - low for v, low in zip(beside(inner_highs, 0), lows)]
        jump_high = [v - high for v, high in zip(beside(inner_lows, 1), highs)]
        square = jnp.zeros_like(theta)
        for b in each:
            square = square + jump_low[b] * jump_low[b] + jump_high[b] * jump_high[b]
            push_low = push_low + mine[b] * jump_low[b]
            push_high = push_high + mine[b] * jump_high[b]
        square_ref[iteration] = square
        own_low = [alpha * jump_low[b] + beta * jump_high[b] for b in each]
        own_high = [beta * jump_low[b] + alpha * jump_high[b] for b in each]
        beyond_low = beside(jump_high, 0)
        beyond_high = beside(jump_low, 1)
    push_ref[0] = c0 * push_low
    push_ref[1] = c0 * push_high


def shards(source, conduct, neighbours, orient):
    blocks = neighbours.shape[0]
    rows, planes, depth = source.shape
    group = lax.axis_size("py") * lax.axis_size("pz")
    all_rows = rows * group
    own_depth = depth // group
    own_block = lax.axis_index("blk")
    member = lax.axis_index("py") * lax.axis_size("pz") + lax.axis_index("pz")
    chosen = jnp.arange(blocks, dtype=jnp.int32) == own_block
    flipped = jnp.sum(jnp.where(chosen, orient, 0)) == 1
    c0, c1, c2 = conduct[0], conduct[1], conduct[2]

    own, forward, mu_plane, box_pick, margin_pick = plane_tables(planes)
    count = forward.shape[1]
    row_ids = np.arange(all_rows)
    local_ids = np.arange(rows)
    depth_ids = np.arange(depth)
    row_basis = jnp.asarray(sine_basis(row_ids, row_ids, all_rows))
    local_basis = jnp.asarray(sine_basis(local_ids, local_ids, rows))
    depth_basis = jnp.asarray(sine_basis(depth_ids, depth_ids, depth))
    beside = np.stack([rows * np.arange(group) - 1, rows * (np.arange(group) + 1)], axis=1)
    beside_basis = sine_basis(beside.reshape(-1), row_ids, all_rows)
    beside_basis = beside_basis.reshape(group, 2, all_rows)
    beside_basis[0, 0] = 0.0
    beside_basis[-1, 1] = 0.0
    beside_basis = jnp.asarray(beside_basis)
    mu_row = jnp.asarray(spectrum(all_rows))
    mu_local = jnp.asarray(spectrum(rows))
    mu_depth = jnp.asarray(spectrum(depth))
    mu_plane = jnp.asarray(mu_plane)
    own_table = jnp.asarray(own)
    first_col, last_col = own_table[0], own_table[-1]
    forward = jnp.asarray(forward)
    forward = jnp.where(flipped, forward[::-1], forward)
    backward = jnp.where(flipped, own_table[::-1], own_table)
    pick = jnp.asarray(box_pick) + c0 * jnp.asarray(margin_pick)

    cells = jnp.einsum("ypz,ym->mpz", source, local_basis, precision=HIGH)
    cells = jnp.einsum("mpz,zk->mpk", cells, depth_basis, precision=HIGH)
    modes = jnp.einsum("mpk,pi->mik", cells, forward, precision=HIGH)
    slab_spectra = (
        c0 * mu_plane[None, :, None]
        + c1 * mu_local[:, None, None]
        + c2 * mu_depth[None, None, :]
    )
    slab = modes / slab_spectra
    edge_first = jnp.sum(slab * local_basis[0][:, None, None], axis=0)
    edge_last = jnp.sum(slab * local_basis[-1][:, None, None], axis=0)
    ends = jnp.einsum("mik,iq->mqk", slab, pick, precision=HIGH)
    plain = jnp.zeros((rows, 2, depth), jnp.float32)
    ends = ends + jnp.concatenate([plain, modes[:, count - 2 :]], axis=1)
    ends = jnp.einsum("mqk,ym->kqy", ends, local_basis, precision=HIGHEST)
    own_squares = jnp.sum(source * source)

    packed = jnp.concatenate(
        [
            jnp.transpose(edge_first),
            jnp.transpose(edge_last)[:, : count - 1],
            jnp.full((depth, 1), own_squares),
            ends.reshape(depth, 4 * rows),
        ],
        axis=1,
    )
    packed = lax.all_to_all(packed, ("py", "pz"), split_axis=0, concat_axis=0, tiled=True)
    packed = packed.reshape(group, own_depth, 2 * count + 4 * rows)
    edge_first = packed[:, :, :count]
    edge_last = packed[:, :, count : 2 * count]
    first_square = jnp.sum(packed[:, 0, 2 * count - 1])
    ends = packed[:, :, 2 * count :].reshape(group, own_depth, 4, rows)

    empty = jnp.zeros_like(edge_first[:1])
    below = jnp.concatenate([empty, edge_last[:-1]], axis=0)
    above = jnp.concatenate([edge_first[1:], empty], axis=0)
    first_rows = row_basis[rows * np.arange(group)]
    last_rows = row_basis[rows * np.arange(group) + rows - 1]
    seam_basis = jnp.concatenate([first_rows, last_rows], axis=0)
    seams = jnp.concatenate([below, above], axis=0)
    joined = c1 * jnp.einsum("rki,rj->kji", seams, seam_basis, precision=HIGH)
    held_depth = lax.dynamic_slice_in_dim(mu_depth, member * own_depth, own_depth)
    cross = c1 * mu_row[None, :] + c2 * held_depth[:, None]
    spectra = c0 * mu_plane[None, None, :] + cross[:, :, None]
    moments = jnp.einsum("kji,iq->qkj", joined / spectra, pick, precision=HIGH)
    moments = moments + jnp.einsum(
        "dkqy,dyj->qkj", ends, row_basis.reshape(group, rows, all_rows), precision=HIGHEST
    )
    shared = jnp.full((1,) + moments.shape[1:], first_square)
    every = lax.all_gather(jnp.concatenate([moments, shared], axis=0), "blk", axis=0)

    half = 0.5 * jnp.sqrt(cross / c0)
    root = jnp.sqrt(1.0 + half * half)
    theta = 2.0 * jnp.log1p(half + half * half / (1.0 + root))
    sinh = 2.0 * half * root
    in_smem = pl.BlockSpec(memory_space=pltpu.SMEM)
    in_vmem = pl.BlockSpec(memory_space=pltpu.VMEM)
    pushes, squares = pl.pallas_call(
        functools.partial(chain_kernel, planes),
        out_shape=(
            jax.ShapeDtypeStruct((2,) + theta.shape, jnp.float32),
            jax.ShapeDtypeStruct((ITERS - 1,) + theta.shape, jnp.float32),
        ),
        in_specs=[in_smem, in_smem, in_smem, in_vmem, in_vmem, in_vmem],
        out_specs=(in_vmem, in_vmem),
        name="chain",
    )(neighbours, own_block.reshape(1), c0.reshape(1), theta, sinh, every)
    squares = c0 * c0 * jnp.sum(squares, axis=(1, 2))

    total = (
        joined[:, :, :planes]
        + pushes[0][:, :, None] * first_col
        + pushes[1][:, :, None] * last_col
    )
    total = total / spectra[:, :, :planes]
    beside_values = jnp.einsum("kji,dsj->dksi", total, beside_basis, precision=HIGH)
    beside_values = beside_values + jnp.stack([below, above], axis=2)[:, :, :, :planes]
    pushes = jnp.einsum(
        "skj,dyj->dksy", pushes, row_basis.reshape(group, rows, all_rows), precision=HIGHEST
    )
    packed = jnp.concatenate(
        [
            beside_values.reshape(group, own_depth, 2 * planes),
            pushes.reshape(group, own_depth, 2 * rows),
            jnp.broadcast_to(squares, (group, own_depth, ITERS - 1)),
        ],
        axis=2,
    ).reshape(depth, 2 * planes + 2 * rows + ITERS - 1)
    packed = lax.all_to_all(packed, ("py", "pz"), split_axis=0, concat_axis=0, tiled=True)
    squares = packed[::own_depth, 2 * planes + 2 * rows :]
    packed = jnp.transpose(packed)
    below = packed[:planes]
    above = packed[planes : 2 * planes]
    pushes = jnp.einsum(
        "syk,ym->smk",
        packed[2 * planes : 2 * planes + 2 * rows].reshape(2, rows, depth),
        local_basis,
        precision=HIGHEST,
    )

    modes = (
        modes[:, :planes]
        + c1 * local_basis[0][:, None, None] * below
        + c1 * local_basis[-1][:, None, None] * above
        + first_col[None, :, None] * pushes[0][:, None, :]
        + last_col[None, :, None] * pushes[1][:, None, :]
    ) / slab_spectra[:, :planes]
    cells = jnp.einsum("mik,ym->yik", modes, local_basis, precision=HIGH)
    cells = jnp.einsum("yik,pi->ypk", cells, backward, precision=HIGH)
    solution = jnp.einsum("ypk,zk->ypz", cells, depth_basis, precision=HIGH)

    cell_count = float(blocks * planes * all_rows * depth)
    sums = jnp.concatenate([jnp.sum(every[:, 4, 0, 0])[None], jnp.sum(squares, axis=0)])
    return (solution, jnp.sqrt(sums / cell_count))


def solution(mesh):
    placed = (P(("py", "pz"), "blk", None), P(), P(), P())
    return jax.shard_map(
        shards,
        mesh=mesh,
        in_specs=placed,
        out_specs=(P(("py", "pz"), "blk", None), P()),
        check_vma=False,
    )
```
